32 devices in a mesh: groups: 2 (over x), agent: 8 (over z, y), tm: 2 (over core).
Axes of the slice: x: 2, y: 2, z: 4, core: 2. Of those that a mesh axis runs over, the one named last changes fastest.
Arguments:
- embedded: bfloat16 [64, 1024, 512], P(('groups', 'tm'), 'agent'), parts along dimension 0, may hold values from -6 to 6
- block_lists: int32 [16, 32, 2], P(('groups', 'agent'), 'tm'), parts along dimension 0, may hold values from 0 to 7, all different within a row; in each aligned block of 16 rows (0 to 15, 16 to 31, ..., all dimensions but the last counted through in order) at most 8 rows name the same one
- done_flags: int32 [64, 1024], P(('groups', 'tm'), 'agent'), parts along dimension 0, may hold values 0 or 1
- rewards: float32 [64, 1024], P(('groups', 'tm'), 'agent'), parts along dimension 0, may hold values from -1.2 to 1.2
- bootstrap: float32 [2048], P(('groups', 'agent')), parts along dimension 0, may hold values from -6 to 6
- agent_proj: bfloat16 [512, 1536], replicated, may hold values from -2 to 2
- agent_merge: bfloat16 [512, 512], replicated, may hold values from -0.75 to 0.75
- time_proj: bfloat16 [512, 1536], replicated, may hold values from -2 to 2
- time_merge: bfloat16 [512, 512], replicated, may hold values from -0.75 to 0.75
- value_weight: float32 [512], replicated, may hold values from -0.25 to 0.25
Outputs:
- values: float32 [64, 1024], P(('groups', 'tm'), 'agent'), parts along dimension 0
- advantages: float32 [64, 1024], P(('groups', 'tm'), 'agent'), parts along dimension 0
The draws below stay inside these ranges and needn't reach their ends.
There are 2 independent parts, one for each index of `groups`. The reference program is written for one: setup_inputs(seed, part) draws one part's arguments, and reference() takes and returns one part's arrays. A program takes and returns all parts, laid end to end along the dimension named above; an argument that names none is the same for every part. Nothing has to cross between parts.
Inputs may be any that keep to these rules, and one draw needn't show every extreme that they name: `block_lists`: each row names 2 different agent blocks. Within the 16 rows of one block along the second dimension no agent block is named more than 8 times, and some agent block is named exactly 8 times.
All inputs are finite; a program needn't handle non-finite values. No bound on the sum of `done_flags` on one device may be relied on, other than what follows from the above.
Results may differ from the reference program's by a relative error of at most 0.0085.
Values may be sent and summed in bfloat16 or wider, within the bound.
A program may use at most 128 MiB of HBM per device.

```python
import math
import jax
import jax.numpy as jnp
import numpy as np
from jax import lax

D = 512
HEADS = 8
HEAD = 64
AGT_DEV = 128
STEPS_DEV = 16
WINDOW = 16
LIST = 2
CAP = 8
BLOCKS = 8
AGENTS = 1024
STEPS = 32


def projection_draw(key):
    queries = jax.random.normal(jax.random.fold_in(key, 11), (D, HEADS, HEAD), jnp.float32) * D ** (-0.5)
    keys_part = jax.random.normal(jax.random.fold_in(key, 12), (D, HEADS, HEAD), jnp.float32) * D ** (-0.5)
    values_part = jax.random.normal(jax.random.fold_in(key, 13), (D, HEADS, HEAD), jnp.float32) * D ** (-0.5)
    stacked = jnp.stack([queries, keys_part, values_part], axis=1)
    stacked = jnp.clip(stacked, -2.0, 2.0)
    return stacked.reshape(D, 3 * D).astype(jnp.bfloat16)


def draw_agent_proj(key, part):
    return projection_draw(jax.random.fold_in(key, 1))


def draw_time_proj(key, part):
    return projection_draw(jax.random.fold_in(key, 2))


def set_ends(values, own_key, smallest, largest):
    longest = values.shape.index(max(values.shape))
    spots = []
    for shift in (0, 1):
        where = [jax.random.randint(jax.random.fold_in(own_key, axis), (), 0, length) for axis, length in enumerate(values.shape)]
        where[longest] = (where[longest] + shift) % values.shape[longest]
        spots.append(tuple(where))
    return values.at[spots[0]].set(smallest).at[spots[1]].set(largest)


def block_scale(rng, shape, split, least, high):
    def one(position, shards_of):
        draws = jax.random.uniform(jax.random.fold_in(jax.random.fold_in(rng, 6), position), (shards_of,), jnp.float32, least / len(split), high / len(split))
        return jnp.repeat(jnp.exp(draws), shape[position] // shards_of).reshape((-1,) + (1,) * (len(shape) - position - 1))

    gain = one(*split[0])
    for cut in split[1:]:
        gain = gain * one(*cut)
    return gain


def assign_block(rng, own, number, rows, amount, top, limit, slope):
    ranking = jax.random.permutation(rng, amount)
    crowded, ordinary = load_shares(amount, rows * top, limit, slope, True), load_shares(amount, rows * top, limit, slope, False)
    places = jnp.arange(amount)

    def named(sizes, offset_by):
        used = int((sizes > 0).sum())
        fixed = max(1, used // 4)
        moved = fixed + (places - fixed + offset_by * (used - fixed)) % max(1, amount - fixed)
        return jnp.zeros((amount,), jnp.int32).at[ranking[jnp.where(places < fixed, places, moved)]].set(jnp.asarray(sizes, jnp.int32))

    sizes = jnp.where(number % 4 == 0, named(crowded, number // 4), named(ordinary, number - number // 4 - 1))
    mixed = jax.random.permutation(jax.random.fold_in(own, 3), amount)
    donor, receiver = mixed[0:amount // 2 * 2:2], mixed[1:amount // 2 * 2:2]
    room = jnp.minimum(sizes[donor] - 1, limit - sizes[receiver]) // 2
    room = jnp.where((donor == ranking[0]) | (receiver == ranking[0]) | (sizes[receiver] == 0), 0, jnp.maximum(room, 0))
    moved = jax.random.randint(jax.random.fold_in(own, 4), (amount // 2,), 0, 1 << 20) % (room + 1)
    sizes = sizes.at[donor].add(-moved).at[receiver].add(moved)
    items = jnp.searchsorted(jnp.cumsum(sizes), jnp.arange(rows * top), side="right").astype(jnp.int32)
    listing = items.reshape(top, rows).T
    listing = listing[jax.random.permutation(jax.random.fold_in(own, 1), rows)]
    offset_by = jax.random.randint(jax.random.fold_in(own, 2), (rows, 1), 0, top)
    return jnp.take_along_axis(listing, (jnp.arange(top)[None, :] + offset_by) % top, axis=1)


def load_shares(amount, total, reach, skew, full):
    portions = [(1 << 20) // math.isqrt(grade ** skew) + 1 for grade in range(1, amount + 1)]
    largest = reach if full else min(reach, max(-(-total // amount), total * portions[0] // sum(portions)))
    least = 1 if total - largest >= amount - 1 else 0
    holding, surplus = [largest] + [least] * (amount - 1), total - largest - least * (amount - 1)
    while surplus > 0:
        movable = [i for i in range(1, amount) if holding[i] < largest] or [i for i in range(1, amount) if holding[i] < reach]
        pool, remaining = sum([portions[i] for i in movable]), surplus
        for i in movable:
            addition = min(reach - holding[i], max(1, remaining * portions[i] // pool), surplus)
            holding[i] = holding[i] + addition
            surplus = surplus - addition
    return np.array(holding)


def normal_values(rng, shape, spread, most, split=(), kind=jnp.bfloat16):
    values = spread * jax.random.normal(rng, shape, jnp.float32)
    if split:
        values = values * block_scale(rng, shape, split, -0.22, 0.18)
    return jnp.clip(values, -most, most).astype(kind)


def setup_inputs(seed: int = 0, part: int = 0) -> dict:
    splits = jax.random.split(jax.random.key(seed), 11)
    part_keys = jax.random.split(jax.random.fold_in(splits[10], part), 11)
    embedded = normal_values(part_keys[0], (STEPS, AGENTS, D), 1.0, 6.0, ((0, 2), (1, 8)))
    block_lists_keys = jax.random.split(jax.random.fold_in(part_keys[1], 1), BLOCKS * STEPS // STEPS_DEV)
    block_lists_turns = jax.random.permutation(jax.random.fold_in(part_keys[1], 3), BLOCKS * STEPS // STEPS_DEV)
    block_lists = jax.vmap(lambda own, number: assign_block(jax.random.fold_in(part_keys[1], 2), own, number, STEPS_DEV, BLOCKS, LIST, CAP, 2))(block_lists_keys, block_lists_turns).reshape((BLOCKS, STEPS, LIST))
    done_flags = set_ends((jax.random.randint(part_keys[2], (STEPS, AGENTS), 0, 32) < 1).astype(jnp.int32), jax.random.fold_in(part_keys[2], 1), 0, 1)
    rewards = normal_values(part_keys[3], (STEPS, AGENTS), 0.2, 1.2, ((0, 2), (1, 8)), jnp.float32)
    bootstrap = normal_values(part_keys[4], (AGENTS,), 1.0, 6.0, ((0, 8),), jnp.float32)
    agent_proj = draw_agent_proj(jax.random.fold_in(splits[10], 71), part)
    agent_merge = normal_values(splits[6], (D, D), HEAD ** -0.5, 0.75)
    time_proj = draw_time_proj(jax.random.fold_in(splits[10], 71), part)
    time_merge = normal_values(splits[8], (D, D), HEAD ** -0.5, 0.75)
    value_weight = normal_values(splits[9], (D,), D ** -0.5, 0.25, (), jnp.float32)
    return {"embedded": embedded, "block_lists": block_lists, "done_flags": done_flags, "rewards": rewards, "bootstrap": bootstrap, "agent_proj": agent_proj, "agent_merge": agent_merge, "time_proj": time_proj, "time_merge": time_merge, "value_weight": value_weight}


discount = 0.9997
trace_decay = 0.995
epsilon = 1e-06

def rms_norm(values):
    return values * lax.rsqrt(lax.optimization_barrier(jnp.mean(values * values, axis=-1, keepdims=True)) + epsilon)

def softmax_rows(scores):
    shifted = scores - lax.optimization_barrier(jnp.max(scores, axis=-1, keepdims=True))
    exponent = jnp.exp(shifted)
    return exponent / lax.optimization_barrier(jnp.sum(exponent, axis=-1, keepdims=True))

def reference(embedded, block_lists, done_flags, rewards, bootstrap, agent_proj, agent_merge, time_proj, time_merge, value_weight):
    tokens = STEPS * AGENTS
    score_scale = HEAD ** (-0.5)
    residual = embedded.astype(jnp.float32).reshape(tokens, D)
    normed = rms_norm(residual).astype(jnp.bfloat16)
    projected = jnp.dot(normed, agent_proj, preferred_element_type=jnp.float32).astype(jnp.bfloat16)
    projected = projected.reshape(STEPS, BLOCKS, AGT_DEV, 3, HEADS, HEAD)

    def agent_step(step):
        step_rows = projected[step]
        listed = step_rows[block_lists[:, step, :]]
        all_keys = jnp.concatenate([step_rows[:, None], listed], axis=1)
        all_keys = all_keys.reshape(BLOCKS, (1 + LIST) * AGT_DEV, 3, HEADS, HEAD)
        queries = step_rows[:, :, 0].astype(jnp.float32)
        scores = jnp.einsum('bqhe,bkhe->bhqk', queries, all_keys[:, :, 1].astype(jnp.float32)) * score_scale
        attention = softmax_rows(scores).astype(jnp.bfloat16)
        attended = jnp.einsum('bhqk,bkhe->bqhe', attention.astype(jnp.float32), all_keys[:, :, 2].astype(jnp.float32))
        return attended.astype(jnp.bfloat16).reshape(AGENTS, D)
    attended = lax.map(agent_step, jnp.arange(STEPS))
    residual = residual + jnp.dot(attended.reshape(tokens, D), agent_merge, preferred_element_type=jnp.float32)
    normed = rms_norm(residual).astype(jnp.bfloat16)
    projected = jnp.dot(normed, time_proj, preferred_element_type=jnp.float32).astype(jnp.bfloat16)
    projected = projected.reshape(STEPS, AGENTS, 3 * D)
    time_keys = projected[:, :, D:]
    padded = jnp.concatenate([jnp.zeros((WINDOW, AGENTS, 2 * D), jnp.bfloat16), time_keys], axis=0)
    block_count = STEPS // WINDOW
    previous = padded[:STEPS].reshape(block_count, WINDOW, AGENTS, 2, HEADS, HEAD)
    current = padded[WINDOW:].reshape(block_count, WINDOW, AGENTS, 2, HEADS, HEAD)
    key_blocks = jnp.concatenate([previous, current], axis=1)
    query_blocks = projected[:, :, :D].reshape(block_count, WINDOW, AGENTS, HEADS, HEAD)
    block_starts = jnp.arange(block_count) * WINDOW

    def time_block(inputs):
        query_block, key_block, start_step = inputs
        query_step = start_step + jnp.arange(WINDOW)
        key_step = start_step - WINDOW + jnp.arange(2 * WINDOW)
        allowed = (key_step[None, :] <= query_step[:, None]) & (key_step[None, :] > query_step[:, None] - WINDOW) & (key_step[None, :] >= 0)
        scores = jnp.einsum('qahe,kahe->ahqk', query_block.astype(jnp.float32), key_block[:, :, 0].astype(jnp.float32)) * score_scale
        scores = jnp.where(allowed[None, None], scores, -1e+30)
        attention = softmax_rows(scores).astype(jnp.bfloat16)
        result = jnp.einsum('ahqk,kahe->qahe', attention.astype(jnp.float32), key_block[:, :, 1].astype(jnp.float32))
        return result.astype(jnp.bfloat16)
    attended = lax.map(time_block, (query_blocks, key_blocks, block_starts))
    residual = residual + jnp.dot(attended.reshape(tokens, D), time_merge, preferred_element_type=jnp.float32)
    values = lax.optimization_barrier(jnp.sum(rms_norm(residual) * value_weight, axis=-1)).reshape(STEPS, AGENTS)
    living = 1.0 - done_flags.astype(jnp.float32)
    following = jnp.concatenate([values[1:], bootstrap[None, :]], axis=0)
    changes = rewards + discount * living * following - values
    factors = discount * trace_decay * living

    def backward(running, inputs):
        change, factor = inputs
        running = change + factor * running
        return (running, running)
    final_carry, advantages = lax.scan(backward, jnp.zeros((AGENTS,), jnp.float32), (changes, factors), reverse=True)
    return (values, advantages)
```

```python
import functools
import math

import jax
import jax.numpy as jnp
from jax import lax
from jax.experimental import pallas as pl
from jax.experimental.pallas import tpu as pltpu
from jax.sharding import PartitionSpec as P

HEADS = 8
WINDOW = 16

discount = 0.9997
trace_decay = 0.995
epsilon = 1e-06
NEG = -1e30
MESH = pl.DeviceIdType.MESH


def normed_bf16(x):
    return (x * lax.rsqrt(jnp.mean(x * x, axis=-1, keepdims=True) + epsilon)).astype(jnp.bfloat16)


def dot(a, b):
    return jnp.dot(a, b, preferred_element_type=jnp.float32)


def pair_attention(q, k, v, head, coef, bias=None):
    rows = q.shape[0]
    first = lax.broadcasted_iota(jnp.int32, q.shape, 1) < head
    zero = jnp.zeros_like(q)
    both = jnp.concatenate([jnp.where(first, q, zero), jnp.where(first, zero, q)], axis=0)
    s = lax.dot_general(both, k, (((1,), (1,)), ((), ())), preferred_element_type=jnp.float32)
    s = s * coef
    if bias is not None:
        s = s + bias
    e = jnp.exp2(s - jnp.max(s, axis=-1, keepdims=True))
    o = dot(e.astype(jnp.bfloat16), v) / jnp.sum(e, axis=-1, keepdims=True)
    return jnp.where(first, o[:rows], o[rows:])


def agent_step(x, listed, proj_ref, merge_ref, tproj_ref, head):
    width = x.shape[-1]
    coef = head**-0.5 * math.log2(math.e)
    x = x.astype(jnp.float32)
    own = dot(normed_bf16(x), proj_ref[...]).astype(jnp.bfloat16)
    other = dot(normed_bf16(listed.astype(jnp.float32)), proj_ref[:, width:]).astype(jnp.bfloat16)
    outs = []
    for lo in range(0, width, 2 * head):
        hi = lo + 2 * head
        k = jnp.concatenate([own[:, width + lo : width + hi], other[:, lo:hi]], axis=0)
        v = jnp.concatenate(
            [own[:, 2 * width + lo : 2 * width + hi], other[:, width + lo : width + hi]], axis=0
        )
        outs.append(pair_attention(own[:, lo:hi], k, v, head, coef))
    mix = jnp.concatenate(outs, axis=1).astype(jnp.bfloat16)
    res = x + dot(mix, merge_ref[...])
    return res, dot(normed_bf16(res), tproj_ref[...]).astype(jnp.bfloat16)


def agent_kernel(head, listing, pos, x_ref, *refs):
    listed = [r[0] for r in refs[:listing]]
    proj, merge, tproj, res_ref, qkv_ref = refs[listing:]
    res, qkv = agent_step(x_ref[0], jnp.concatenate(listed, axis=0), proj, merge, tproj, head)
    res_ref[0] = res
    qkv_ref[0] = qkv


def agent_call(embedded, arrived, positions, proj, merge, tproj, head):
    steps, agents, width = embedded.shape
    listing = positions.shape[0] // steps
    block = (1, agents, width)
    whole = lambda a: pl.BlockSpec(a.shape, lambda t, p: (0, 0))
    pick = lambda j: pl.BlockSpec(block, lambda t, p: (p[t * listing + j], 0, 0))
    return pl.pallas_call(
        functools.partial(agent_kernel, head, listing),
        grid_spec=pltpu.PrefetchScalarGridSpec(
            num_scalar_prefetch=1,
            grid=(steps,),
            in_specs=[pl.BlockSpec(block, lambda t, p: (t, 0, 0))]
            + [pick(j) for j in range(listing)]
            + [whole(proj), whole(merge), whole(tproj)],
            out_specs=[
                pl.BlockSpec(block, lambda t, p: (t, 0, 0)),
                pl.BlockSpec((1, agents, 3 * width), lambda t, p: (t, 0, 0)),
            ],
        ),
        out_shape=[
            jax.ShapeDtypeStruct((steps, agents, width), jnp.float32),
            jax.ShapeDtypeStruct((steps, agents, 3 * width), jnp.bfloat16),
        ],
        compiler_params=pltpu.CompilerParams(vmem_limit_bytes=40 * 2**20),
        name="agent_attention",
    )(positions, embedded, *([arrived] * listing), proj, merge, tproj)


def time_kernel(head, res_ref, qkv_ref, prev_ref, merge_ref, weight_ref, out_ref, mix_ref):
    steps, agents, width = res_ref.shape
    coef = head**-0.5 * math.log2(math.e)
    oct_ = 8
    rows, cols = steps * oct_, 2 * steps * oct_
    r = lax.broadcasted_iota(jnp.int32, (rows, cols), 0)
    c = lax.broadcasted_iota(jnp.int32, (rows, cols), 1)
    qt, ks = r // oct_, c // oct_ - steps
    seen = (ks <= qt) & (ks > qt - WINDOW) & ((ks >= 0) | (lax.axis_index("tm") > 0))
    bias = jnp.where(seen & (r % oct_ == c % oct_), 0.0, NEG).astype(jnp.float32)
    bias = jnp.concatenate([bias, bias], axis=0)

    def halves(block):
        block = block.astype(jnp.float32)
        return [
            block[:, h : h + oct_].reshape(steps * oct_, block.shape[-1]).astype(jnp.bfloat16)
            for h in (0, oct_)
        ]

    def group(i, _):
        at = pl.ds(pl.multiple_of(i * 2 * oct_, 2 * oct_), 2 * oct_)
        for lo in range(0, width, 2 * head):
            hi = lo + 2 * head
            q = halves(qkv_ref[:, at, lo:hi])
            k0 = halves(prev_ref[:, at, lo:hi])
            k1 = halves(qkv_ref[:, at, width + lo : width + hi])
            v0 = halves(prev_ref[:, at, width + lo : width + hi])
            v1 = halves(qkv_ref[:, at, 2 * width + lo : 2 * width + hi])
            outs = []
            for h in range(2):
                k = jnp.concatenate([k0[h], k1[h]], axis=0)
                v = jnp.concatenate([v0[h], v1[h]], axis=0)
                o = pair_attention(q[h], k, v, head, coef, bias)
                outs.append(o.reshape(steps, oct_, hi - lo))
            mix_ref[:, at, lo:hi] = jnp.concatenate(outs, axis=1).astype(jnp.bfloat16)
        return 0

    lax.fori_loop(0, agents // (2 * oct_), group, 0)

    def finish(t, _):
        res = res_ref[t] + dot(mix_ref[t], merge_ref[...])
        square = res * res
        scaled = res * weight_ref[...]
        lanes = 128
        sq = sum(square[:, j : j + lanes] for j in range(0, width, lanes))
        sc = sum(scaled[:, j : j + lanes] for j in range(0, width, lanes))
        mean = jnp.sum(sq.T, axis=0, keepdims=True) / width
        out_ref[pl.ds(t, 1), :] = jnp.sum(sc.T, axis=0, keepdims=True) * lax.rsqrt(mean + epsilon)
        return 0

    lax.fori_loop(0, steps, finish, 0)


def time_call(res, qkv, prev, merge, weight, head):
    steps, agents, width = res.shape
    return pl.pallas_call(
        functools.partial(time_kernel, head),
        out_shape=jax.ShapeDtypeStruct((steps, agents), jnp.float32),
        in_specs=[pl.BlockSpec(memory_space=pltpu.VMEM)] * 5,
        out_specs=pl.BlockSpec(memory_space=pltpu.VMEM),
        scratch_shapes=[pltpu.VMEM((steps, agents, width), jnp.bfloat16)],
        compiler_params=pltpu.CompilerParams(vmem_limit_bytes=56 * 2**20),
        name="time_attention",
    )(res, qkv, prev, merge, weight.reshape(1, width))


def from_behind(value, axis, by):
    devices = lax.axis_size(axis)
    pairs = [(i, i + by) for i in range(devices) if 0 <= i + by < devices]
    return lax.ppermute(value, axis, pairs)


def advantage_pass(values, done_flags, rewards, bootstrap):
    steps = values.shape[0]
    parts = lax.axis_size("tm")
    last = lax.axis_index("tm") == parts - 1
    living = 1.0 - done_flags.astype(jnp.float32)
    factors = discount * trace_decay * living

    def run(following_last, running):
        following = jnp.concatenate([values[1:], following_last[None]], axis=0)
        changes = rewards + discount * living * following - values
        rows = [None] * steps
        for t in reversed(range(steps)):
            running = changes[t] + factors[t] * running
            rows[t] = running
        return jnp.stack(rows)

    zero = jnp.zeros_like(bootstrap)
    advantages = run(bootstrap, zero)
    for _ in range(parts - 1):
        sent = jnp.stack([values[0], advantages[0]])
        got = from_behind(sent, "tm", -1)
        advantages = run(jnp.where(last, bootstrap, got[0]), jnp.where(last, zero, got[1]))
    return advantages


def exchange(embedded, block_lists):
    steps, agents, width = embedded.shape
    listing = block_lists.shape[2]
    blocks = lax.axis_size("agent")
    capacity = max(2, (2 * steps * listing + blocks - 1) // blocks)
    peers = block_lists[0].reshape(-1)
    count = peers.shape[0]
    row_steps = jnp.arange(count, dtype=jnp.int32) // listing
    hits = (peers[:, None] == jnp.arange(blocks, dtype=jnp.int32)[None, :]).astype(jnp.int32)
    earlier = jnp.cumsum(hits, axis=0) - hits
    slot = jnp.sum(earlier * hits, axis=1)
    slots = (slot[:, None] == jnp.arange(capacity, dtype=jnp.int32)[None, :]).astype(jnp.int32)
    requests = jnp.sum((hits * row_steps[:, None])[:, :, None] * slots[:, None, :], axis=0)
    wanted = lax.all_to_all(requests, "agent", split_axis=0, concat_axis=0, tiled=True)
    outgoing = embedded[wanted.reshape(-1)].reshape(blocks, capacity, agents, width)
    arrived = lax.all_to_all(outgoing, "agent", split_axis=0, concat_axis=0, tiled=True)
    return arrived.reshape(blocks * capacity, agents, width), peers * capacity + slot


def body(
    embedded,
    block_lists,
    done_flags,
    rewards,
    bootstrap,
    agent_proj,
    agent_merge,
    time_proj,
    time_merge,
    value_weight,
):
    steps, agents, width = embedded.shape
    head = width // HEADS
    assert steps == WINDOW
    arrived, positions = exchange(embedded, block_lists)
    res, qkv = agent_call(embedded, arrived, positions, agent_proj, agent_merge, time_proj, head)
    prev = from_behind(qkv[:, :, width:], "tm", 1)
    values = time_call(res, qkv, prev, time_merge, value_weight, head)
    return (values, advantage_pass(values, done_flags, rewards, bootstrap))


def solution(mesh):
    placed = (
        P(("groups", "tm"), "agent", None),
        P(("groups", "agent"), "tm", None),
        P(("groups", "tm"), "agent"),
        P(("groups", "tm"), "agent"),
        P(("groups", "agent")),
        P(),
        P(),
        P(),
        P(),
        P(),
    )
    return jax.shard_map(
        body,
        mesh=mesh,
        in_specs=placed,
        out_specs=(P(("groups", "tm"), "agent"), P(("groups", "tm"), "agent")),
        check_vma=False,
    )
```

```python
import functools
import math

import jax
import jax.numpy as jnp
from jax import lax
from jax.experimental import pallas as pl
from jax.experimental.pallas import tpu as pltpu
from jax.sharding import PartitionSpec as P

HEADS = 8
WINDOW = 16

discount = 0.9997
trace_decay = 0.995
epsilon = 1e-06
NEG = -1e30
MESH = pl.DeviceIdType.MESH


def normed_bf16(x):
    return (x * lax.rsqrt(jnp.mean(x * x, axis=-1, keepdims=True) + epsilon)).astype(jnp.bfloat16)


def dot(a, b):
    return jnp.dot(a, b, preferred_element_type=jnp.float32)


def pair_attention(q, k, v, head, coef, bias=None):
    rows = q.shape[0]
    first = lax.broadcasted_iota(jnp.int32, q.shape, 1) < head
    zero = jnp.zeros_like(q)
    both = jnp.concatenate([jnp.where(first, q, zero), jnp.where(first, zero, q)], axis=0)
    s = lax.dot_general(both, k, (((1,), (1,)), ((), ())), preferred_element_type=jnp.float32)
    s = s * coef
    if bias is not None:
        s = s + bias
    e = jnp.exp2(s - jnp.max(s, axis=-1, keepdims=True))
    o = dot(e.astype(jnp.bfloat16), v) / jnp.sum(e, axis=-1, keepdims=True)
    return jnp.where(first, o[:rows], o[rows:])


def agent_step(x, listed, proj_ref, merge_ref, tproj_ref, head):
    width = x.shape[-1]
    coef = head**-0.5 * math.log2(math.e)
    x = x.astype(jnp.float32)
    own = dot(normed_bf16(x), proj_ref[...]).astype(jnp.bfloat16)
    other = dot(normed_bf16(listed.astype(jnp.float32)), proj_ref[:, width:]).astype(jnp.bfloat16)
    outs = []
    for lo in range(0, width, 2 * head):
        hi = lo + 2 * head
        k = jnp.concatenate([own[:, width + lo : width + hi], other[:, lo:hi]], axis=0)
        v = jnp.concatenate(
            [own[:, 2 * width + lo : 2 * width + hi], other[:, width + lo : width + hi]], axis=0
        )
        outs.append(pair_attention(own[:, lo:hi], k, v, head, coef))
    mix = jnp.concatenate(outs, axis=1).astype(jnp.bfloat16)
    res = x + dot(mix, merge_ref[...])
    return res, dot(normed_bf16(res), tproj_ref[...]).astype(jnp.bfloat16)


def agent_kernel(head, listing, pos, x_ref, *refs):
    listed = [r[0] for r in refs[:listing]]
    proj, merge, tproj, res_ref, qkv_ref = refs[listing:]
    res, qkv = agent_step(x_ref[0], jnp.concatenate(listed, axis=0), proj, merge, tproj, head)
    res_ref[0] = res
    qkv_ref[0] = qkv


def agent_call(embedded, arrived, positions, proj, merge, tproj, head):
    steps, agents, width = embedded.shape
    listing = positions.shape[0] // steps
    block = (1, agents, width)
    whole = lambda a: pl.BlockSpec(a.shape, lambda t, p: (0, 0))
    pick = lambda j: pl.BlockSpec(block, lambda t, p: (p[t * listing + j], 0, 0))
    return pl.pallas_call(
        functools.partial(agent_kernel, head, listing),
        grid_spec=pltpu.PrefetchScalarGridSpec(
            num_scalar_prefetch=1,
            grid=(steps,),
            in_specs=[pl.BlockSpec(block, lambda t, p: (t, 0, 0))]
            + [pick(j) for j in range(listing)]
            + [whole(proj), whole(merge), whole(tproj)],
            out_specs=[
                pl.BlockSpec(block, lambda t, p: (t, 0, 0)),
                pl.BlockSpec((1, agents, 3 * width), lambda t, p: (t, 0, 0)),
            ],
        ),
        out_shape=[
            jax.ShapeDtypeStruct((steps, agents, width), jnp.float32),
            jax.ShapeDtypeStruct((steps, agents, 3 * width), jnp.bfloat16),
        ],
        compiler_params=pltpu.CompilerParams(vmem_limit_bytes=40 * 2**20),
        name="agent_attention",
    )(positions, embedded, *([arrived] * listing), proj, merge, tproj)


def time_kernel(head, res_ref, qkv_ref, prev_ref, merge_ref, weight_ref, out_ref, mix_ref):
    steps, agents, width = res_ref.shape
    coef = head**-0.5 * math.log2(math.e)
    oct_ = 8
    rows, cols = steps * oct_, 2 * steps * oct_
    r = lax.broadcasted_iota(jnp.int32, (rows, cols), 0)
    c = lax.broadcasted_iota(jnp.int32, (rows, cols), 1)
    qt, ks = r // oct_, c // oct_ - steps
    seen = (ks <= qt) & (ks > qt - WINDOW) & ((ks >= 0) | (lax.axis_index("tm") > 0))
    bias = jnp.where(seen & (r % oct_ == c % oct_), 0.0, NEG).astype(jnp.float32)
    bias = jnp.concatenate([bias, bias], axis=0)

    def halves(block):
        block = block.astype(jnp.float32)
        return [
            block[:, h : h + oct_].reshape(steps * oct_, block.shape[-1]).astype(jnp.bfloat16)
            for h in (0, oct_)
        ]

    def group(i, _):
        at = pl.ds(pl.multiple_of(i * 2 * oct_, 2 * oct_), 2 * oct_)
        for lo in range(0, width, 2 * head):
            hi = lo + 2 * head
            q = halves(qkv_ref[:, at, lo:hi])
            k0 = halves(prev_ref[:, at, lo:hi])
            k1 = halves(qkv_ref[:, at, width + lo : width + hi])
            v0 = halves(prev_ref[:, at, width + lo : width + hi])
            v1 = halves(qkv_ref[:, at, 2 * width + lo : 2 * width + hi])
            outs = []
            for h in range(2):
                k = jnp.concatenate([k0[h], k1[h]], axis=0)
                v = jnp.concatenate([v0[h], v1[h]], axis=0)
                o = pair_attention(q[h], k, v, head, coef, bias)
                outs.append(o.reshape(steps, oct_, hi - lo))
            mix_ref[:, at, lo:hi] = jnp.concatenate(outs, axis=1).astype(jnp.bfloat16)
        return 0

    lax.fori_loop(0, agents // (2 * oct_), group, 0)

    def finish(t, _):
        res = res_ref[t] + dot(mix_ref[t], merge_ref[...])
        square = res * res
        scaled = res * weight_ref[...]
        lanes = 128
        sq = sum(square[:, j : j + lanes] for j in range(0, width, lanes))
        sc = sum(scaled[:, j : j + lanes] for j in range(0, width, lanes))
        mean = jnp.sum(sq.T, axis=0, keepdims=True) / width
        out_ref[pl.ds(t, 1), :] = jnp.sum(sc.T, axis=0, keepdims=True) * lax.rsqrt(mean + epsilon)
        return 0

    lax.fori_loop(0, steps, finish, 0)


def time_call(res, qkv, prev, merge, weight, head):
    steps, agents, width = res.shape
    return pl.pallas_call(
        functools.partial(time_kernel, head),
        out_shape=jax.ShapeDtypeStruct((steps, agents), jnp.float32),
        in_specs=[pl.BlockSpec(memory_space=pltpu.VMEM)] * 5,
        out_specs=pl.BlockSpec(memory_space=pltpu.VMEM),
        scratch_shapes=[pltpu.VMEM((steps, agents, width), jnp.bfloat16)],
        compiler_params=pltpu.CompilerParams(vmem_limit_bytes=56 * 2**20),
        name="time_attention",
    )(res, qkv, prev, merge, weight.reshape(1, width))


def from_behind(value, axis, by):
    devices = lax.axis_size(axis)
    pairs = [(i, i + by) for i in range(devices) if 0 <= i + by < devices]
    return lax.ppermute(value, axis, pairs)


def advantage_pass(values, done_flags, rewards, bootstrap):
    steps = values.shape[0]
    parts = lax.axis_size("tm")
    last = lax.axis_index("tm") == parts - 1
    living = 1.0 - done_flags.astype(jnp.float32)
    factors = discount * trace_decay * living

    def run(following_last, running):
        following = jnp.concatenate([values[1:], following_last[None]], axis=0)
        changes = rewards + discount * living * following - values
        rows = [None] * steps
        for t in reversed(range(steps)):
            running = changes[t] + factors[t] * running
            rows[t] = running
        return jnp.stack(rows)

    zero = jnp.zeros_like(bootstrap)
    advantages = run(bootstrap, zero)
    for _ in range(parts - 1):
        sent = jnp.stack([values[0], advantages[0]])
        got = from_behind(sent, "tm", -1)
        advantages = run(jnp.where(last, bootstrap, got[0]), jnp.where(last, zero, got[1]))
    return advantages


def exchange(embedded, block_lists):
    steps, agents, width = embedded.shape
    listing = block_lists.shape[2]
    blocks = lax.axis_size("agent")
    capacity = max(2, (2 * steps * listing + blocks - 1) // blocks)
    peers = block_lists[0].reshape(-1)
    count = peers.shape[0]
    row_steps = jnp.arange(count, dtype=jnp.int32) // listing
    hits = (peers[:, None] == jnp.arange(blocks, dtype=jnp.int32)[None, :]).astype(jnp.int32)
    earlier = jnp.cumsum(hits, axis=0) - hits
    slot = jnp.sum(earlier * hits, axis=1)
    slots = (slot[:, None] == jnp.arange(capacity, dtype=jnp.int32)[None, :]).astype(jnp.int32)
    requests = jnp.sum((hits * row_steps[:, None])[:, :, None] * slots[:, None, :], axis=0)
    wanted = lax.all_to_all(requests, "agent", split_axis=0, concat_axis=0, tiled=True)
    outgoing = embedded[wanted.reshape(-1)].reshape(blocks, capacity, agents, width)
    arrived = lax.all_to_all(outgoing, "agent", split_axis=0, concat_axis=0, tiled=True)
    return arrived.reshape(blocks * capacity, agents, width), peers * capacity + slot


LEAD = 2


def row_gather_kernel(
    head, x_ref, mine_ref, theirs_ref, proj, merge, tproj, res_ref, qkv_ref,
    row, yout, yin, send_sem, recv_sem, ysend, yrecv,
):
    steps = x_ref.shape[0]
    listing = mine_ref.shape[1]
    lines = row.shape[0]
    me = lax.axis_index("agent")
    y = lax.rem(me, 2)
    z = lax.div(me, 2)
    across = me + 1 - 2 * y
    has_up, has_down = z < lines - 1, z > 0
    up, down = {"agent": me + 2}, {"agent": me - 2}

    barrier = pltpu.get_barrier_semaphore()
    pl.semaphore_signal(barrier, inc=1, device_id={"agent": across}, device_id_type=MESH)

    @pl.when(has_up)
    def _():
        pl.semaphore_signal(barrier, inc=1, device_id=up, device_id_type=MESH)

    @pl.when(has_down)
    def _():
        pl.semaphore_signal(barrier, inc=1, device_id=down, device_id_type=MESH)

    pl.semaphore_wait(barrier, 1 + has_up.astype(jnp.int32) + has_down.astype(jnp.int32))

    def hop(way, h, c, own=False):
        origin = z - h if way == 0 else z + h
        return pltpu.make_async_remote_copy(
            src_ref=x_ref.at[c] if own else row.at[origin, c],
            dst_ref=row.at[origin, c],
            send_sem=send_sem.at[way, h, c],
            recv_sem=recv_sem.at[way, h, c],
            device_id=up if way == 0 else down,
            device_id_type=MESH,
        )

    def arrival(way, h, c):
        origin = z - h if way == 0 else z + h
        return pltpu.make_async_remote_copy(
            src_ref=row.at[origin, c],
            dst_ref=row.at[origin, c],
            send_sem=send_sem.at[way, h - 1, c],
            recv_sem=recv_sem.at[way, h - 1, c],
            device_id={"agent": across},
            device_id_type=MESH,
        )

    def crossing(c):
        return pltpu.make_async_remote_copy(
            src_ref=yout.at[c],
            dst_ref=yin.at[c],
            send_sem=ysend.at[c],
            recv_sem=yrecv.at[c],
            device_id={"agent": across},
            device_id_type=MESH,
        )

    def held(way, h):
        return z >= h if way == 0 else z + h < lines

    def sends(way, h):
        return held(way, h) & (has_up if way == 0 else has_down)

    def start_own(c):
        for way in range(2):
            @pl.when(sends(way, 0) & (c < steps))
            def _(way=way):
                hop(way, 0, c, own=True).start()

    for c in range(LEAD):
        start_own(c)

    def fill(t, _):
        row[z, t] = x_ref[t]
        return 0

    lax.fori_loop(0, steps, fill, 0)

    def pick(idx, t, other):
        for zz in range(lines):
            other = jnp.where(idx == 2 * zz + y, row[zz, t], other)
        return other

    def iteration(i, _):
        start_own(i + LEAD)
        for h in range(1, lines):
            c = i - h
            for way in range(2):
                @pl.when((c >= 0) & (c < steps) & held(way, h))
                def _(way=way, h=h, c=c):
                    arrival(way, h, c).wait_recv()

                if h < lines - 1:
                    @pl.when((c >= 0) & (c < steps) & sends(way, h))
                    def _(way=way, h=h, c=c):
                        hop(way, h, c).start()
        c = i - (lines - 1)

        @pl.when((c >= 0) & (c < steps))
        def _():
            for j in range(listing):
                yout[c, j] = pick(theirs_ref[c, j], c, row[0, c])
            crossing(c).start()

        t = i - lines

        @pl.when((t >= 0) & (t < steps))
        def _():
            crossing(t).wait_recv()
            listed = [pick(mine_ref[t, j], t, yin[t, j]) for j in range(listing)]
            res, qkv = agent_step(x_ref[t], jnp.concatenate(listed, axis=0), proj, merge, tproj, head)
            res_ref[t] = res
            qkv_ref[t] = qkv

        return 0

    lax.fori_loop(0, steps + lines, iteration, 0)

    def drain(c, _):
        crossing(c).wait_send()
        for way in range(2):
            for h in range(lines - 1):
                @pl.when(sends(way, h))
                def _(way=way, h=h):
                    hop(way, h, c, own=h == 0).wait_send()
        return 0

    lax.fori_loop(0, steps, drain, 0)


def row_gather_call(embedded, mine, theirs, proj, merge, tproj, head):
    steps, agents, width = embedded.shape
    lines = lax.axis_size("agent") // 2
    listing = mine.shape[1]
    vmem, smem = pl.BlockSpec(memory_space=pltpu.VMEM), pl.BlockSpec(memory_space=pltpu.SMEM)
    return pl.pallas_call(
        functools.partial(row_gather_kernel, head),
        in_specs=[vmem, smem, smem, vmem, vmem, vmem],
        out_specs=[vmem, vmem],
        out_shape=[
            jax.ShapeDtypeStruct((steps, agents, width), jnp.float32),
            jax.ShapeDtypeStruct((steps, agents, 3 * width), jnp.bfloat16),
        ],
        scratch_shapes=[
            pltpu.VMEM((lines, steps, agents, width), jnp.bfloat16),
            pltpu.VMEM((steps, listing, agents, width), jnp.bfloat16),
            pltpu.VMEM((steps, listing, agents, width), jnp.bfloat16),
            pltpu.SemaphoreType.DMA((2, lines - 1, steps)),
            pltpu.SemaphoreType.DMA((2, lines - 1, steps)),
            pltpu.SemaphoreType.DMA((steps,)),
            pltpu.SemaphoreType.DMA((steps,)),
        ],
        compiler_params=pltpu.CompilerParams(
            collective_id=0, has_side_effects=True, vmem_limit_bytes=58 * 2**20
        ),
        name="row_gather_attention",
    )(embedded, mine, theirs, proj, merge, tproj)


def body(
    embedded,
    block_lists,
    done_flags,
    rewards,
    bootstrap,
    agent_proj,
    agent_merge,
    time_proj,
    time_merge,
    value_weight,
):
    steps, agents, width = embedded.shape
    head = width // HEADS
    assert steps == WINDOW
    blocks = lax.axis_size("agent")
    gathered = (blocks // 2) * steps * agents * width * 2
    if blocks % 2 == 0 and blocks > 2 and gathered <= 12 * 2**20:
        theirs = lax.ppermute(block_lists[0], "agent", [(i, i ^ 1) for i in range(blocks)])
        res, qkv = row_gather_call(
            embedded, block_lists[0], theirs, agent_proj, agent_merge, time_proj, head
        )
    else:
        arrived, positions = exchange(embedded, block_lists)
        res, qkv = agent_call(
            embedded, arrived, positions, agent_proj, agent_merge, time_proj, head
        )
    prev = from_behind(qkv[:, :, width:], "tm", 1)
    values = time_call(res, qkv, prev, time_merge, value_weight, head)
    return (values, advantage_pass(values, done_flags, rewards, bootstrap))


def solution(mesh):
    placed = (
        P(("groups", "tm"), "agent", None),
        P(("groups", "agent"), "tm", None),
        P(("groups", "tm"), "agent"),
        P(("groups", "tm"), "agent"),
        P(("groups", "agent")),
        P(),
        P(),
        P(),
        P(),
        P(),
    )
    return jax.shard_map(
        body,
        mesh=mesh,
        in_specs=placed,
        out_specs=(P(("groups", "tm"), "agent"), P(("groups", "tm"), "agent")),
        check_vma=False,
    )
```

```python
import functools
import math

import jax
import jax.numpy as jnp
from jax import lax
from jax.experimental import pallas as pl
from jax.experimental.pallas import tpu as pltpu
from jax.sharding import PartitionSpec as P

HEADS = 8
WINDOW = 16

discount = 0.9997
trace_decay = 0.995
epsilon = 1e-06
NEG = -1e30
MESH = pl.DeviceIdType.MESH


def normed_bf16(x):
    return (x * lax.rsqrt(jnp.mean(x * x, axis=-1, keepdims=True) + epsilon)).astype(jnp.bfloat16)


def dot(a, b):
    return jnp.dot(a, b, preferred_element_type=jnp.float32)


def pair_attention(q, k, v, head, coef, bias=None):
    rows = q.shape[0]
    first = lax.broadcasted_iota(jnp.int32, q.shape, 1) < head
    zero = jnp.zeros_like(q)
    both = jnp.concatenate([jnp.where(first, q, zero), jnp.where(first, zero, q)], axis=0)
    s = lax.dot_general(both, k, (((1,), (1,)), ((), ())), preferred_element_type=jnp.float32)
    s = s * coef
    if bias is not None:
        s = s + bias
    e = jnp.exp2(s - jnp.max(s, axis=-1, keepdims=True))
    o = dot(e.astype(jnp.bfloat16), v) / jnp.sum(e, axis=-1, keepdims=True)
    return jnp.where(first, o[:rows], o[rows:])


def agent_step(x, listed, proj_ref, merge_ref, tproj_ref, head):
    width = x.shape[-1]
    coef = head**-0.5 * math.log2(math.e)
    x = x.astype(jnp.float32)
    own = dot(normed_bf16(x), proj_ref[...]).astype(jnp.bfloat16)
    other = dot(normed_bf16(listed.astype(jnp.float32)), proj_ref[:, width:]).astype(jnp.bfloat16)
    outs = []
    for lo in range(0, width, 2 * head):
        hi = lo + 2 * head
        k = jnp.concatenate([own[:, width + lo : width + hi], other[:, lo:hi]], axis=0)
        v = jnp.concatenate(
            [own[:, 2 * width + lo : 2 * width + hi], other[:, width + lo : width + hi]], axis=0
        )
        outs.append(pair_attention(own[:, lo:hi], k, v, head, coef))
    mix = jnp.concatenate(outs, axis=1).astype(jnp.bfloat16)
    res = x + dot(mix, merge_ref[...])
    return res, dot(normed_bf16(res), tproj_ref[...]).astype(jnp.bfloat16)


def agent_kernel(head, listing, pos, x_ref, *refs):
    listed = [r[0] for r in refs[:listing]]
    proj, merge, tproj, res_ref, qkv_ref = refs[listing:]
    res, qkv = agent_step(x_ref[0], jnp.concatenate(listed, axis=0), proj, merge, tproj, head)
    res_ref[0] = res
    qkv_ref[0] = qkv


def agent_call(embedded, arrived, positions, proj, merge, tproj, head):
    steps, agents, width = embedded.shape
    listing = positions.shape[0] // steps
    block = (1, agents, width)
    whole = lambda a: pl.BlockSpec(a.shape, lambda t, p: (0, 0))
    pick = lambda j: pl.BlockSpec(block, lambda t, p: (p[t * listing + j], 0, 0))
    return pl.pallas_call(
        functools.partial(agent_kernel, head, listing),
        grid_spec=pltpu.PrefetchScalarGridSpec(
            num_scalar_prefetch=1,
            grid=(steps,),
            in_specs=[pl.BlockSpec(block, lambda t, p: (t, 0, 0))]
            + [pick(j) for j in range(listing)]
            + [whole(proj), whole(merge), whole(tproj)],
            out_specs=[
                pl.BlockSpec(block, lambda t, p: (t, 0, 0)),
                pl.BlockSpec((1, agents, 3 * width), lambda t, p: (t, 0, 0)),
            ],
        ),
        out_shape=[
            jax.ShapeDtypeStruct((steps, agents, width), jnp.float32),
            jax.ShapeDtypeStruct((steps, agents, 3 * width), jnp.bfloat16),
        ],
        compiler_params=pltpu.CompilerParams(vmem_limit_bytes=40 * 2**20),
        name="agent_attention",
    )(positions, embedded, *([arrived] * listing), proj, merge, tproj)


def time_kernel(head, res_ref, qkv_ref, prev_ref, merge_ref, weight_ref, out_ref, mix_ref):
    steps, agents, width = res_ref.shape
    coef = head**-0.5 * math.log2(math.e)
    oct_ = 8
    rows, cols = steps * oct_, 2 * steps * oct_
    r = lax.broadcasted_iota(jnp.int32, (rows, cols), 0)
    c = lax.broadcasted_iota(jnp.int32, (rows, cols), 1)
    qt, ks = r // oct_, c // oct_ - steps
    seen = (ks <= qt) & (ks > qt - WINDOW) & ((ks >= 0) | (lax.axis_index("tm") > 0))
    bias = jnp.where(seen & (r % oct_ == c % oct_), 0.0, NEG).astype(jnp.float32)
    bias = jnp.concatenate([bias, bias], axis=0)

    def halves(block):
        block = block.astype(jnp.float32)
        return [
            block[:, h : h + oct_].reshape(steps * oct_, block.shape[-1]).astype(jnp.bfloat16)
            for h in (0, oct_)
        ]

    def group(i, _):
        at = pl.ds(pl.multiple_of(i * 2 * oct_, 2 * oct_), 2 * oct_)
        for lo in range(0, width, 2 * head):
            hi = lo + 2 * head
            q = halves(qkv_ref[:, at, lo:hi])
            k0 = halves(prev_ref[:, at, lo:hi])
            k1 = halves(qkv_ref[:, at, width + lo : width + hi])
            v0 = halves(prev_ref[:, at, width + lo : width + hi])
            v1 = halves(qkv_ref[:, at, 2 * width + lo : 2 * width + hi])
            outs = []
            for h in range(2):
                k = jnp.concatenate([k0[h], k1[h]], axis=0)
                v = jnp.concatenate([v0[h], v1[h]], axis=0)
                o = pair_attention(q[h], k, v, head, coef, bias)
                outs.append(o.reshape(steps, oct_, hi - lo))
            mix_ref[:, at, lo:hi] = jnp.concatenate(outs, axis=1).astype(jnp.bfloat16)
        return 0

    lax.fori_loop(0, agents // (2 * oct_), group, 0)

    def finish(t, _):
        res = res_ref[t] + dot(mix_ref[t], merge_ref[...])
        square = res * res
        scaled = res * weight_ref[...]
        lanes = 128
        sq = sum(square[:, j : j + lanes] for j in range(0, width, lanes))
        sc = sum(scaled[:, j : j + lanes] for j in range(0, width, lanes))
        mean = jnp.sum(sq.T, axis=0, keepdims=True) / width
        out_ref[pl.ds(t, 1), :] = jnp.sum(sc.T, axis=0, keepdims=True) * lax.rsqrt(mean + epsilon)
        return 0

    lax.fori_loop(0, steps, finish, 0)


def time_call(res, qkv, prev, merge, weight, head):
    steps, agents, width = res.shape
    return pl.pallas_call(
        functools.partial(time_kernel, head),
        out_shape=jax.ShapeDtypeStruct((steps, agents), jnp.float32),
        in_specs=[pl.BlockSpec(memory_space=pltpu.VMEM)] * 5,
        out_specs=pl.BlockSpec(memory_space=pltpu.VMEM),
        scratch_shapes=[pltpu.VMEM((steps, agents, width), jnp.bfloat16)],
        compiler_params=pltpu.CompilerParams(vmem_limit_bytes=56 * 2**20),
        name="time_attention",
    )(res, qkv, prev, merge, weight.reshape(1, width))


def from_behind(value, axis, by):
    devices = lax.axis_size(axis)
    pairs = [(i, i + by) for i in range(devices) if 0 <= i + by < devices]
    return lax.ppermute(value, axis, pairs)


def advantage_pass(values, done_flags, rewards, bootstrap):
    steps = values.shape[0]
    parts = lax.axis_size("tm")
    last = lax.axis_index("tm") == parts - 1
    living = 1.0 - done_flags.astype(jnp.float32)
    factors = discount * trace_decay * living

    def run(following_last, running):
        following = jnp.concatenate([values[1:], following_last[None]], axis=0)
        changes = rewards + discount * living * following - values
        rows = [None] * steps
        for t in reversed(range(steps)):
            running = changes[t] + factors[t] * running
            rows[t] = running
        return jnp.stack(rows)

    zero = jnp.zeros_like(bootstrap)
    advantages = run(bootstrap, zero)
    for _ in range(parts - 1):
        sent = jnp.stack([values[0], advantages[0]])
        got = from_behind(sent, "tm", -1)
        advantages = run(jnp.where(last, bootstrap, got[0]), jnp.where(last, zero, got[1]))
    return advantages


def exchange(embedded, block_lists):
    steps, agents, width = embedded.shape
    listing = block_lists.shape[2]
    blocks = lax.axis_size("agent")
    capacity = max(2, (2 * steps * listing + blocks - 1) // blocks)
    peers = block_lists[0].reshape(-1)
    count = peers.shape[0]
    row_steps = jnp.arange(count, dtype=jnp.int32) // listing
    hits = (peers[:, None] == jnp.arange(blocks, dtype=jnp.int32)[None, :]).astype(jnp.int32)
    earlier = jnp.cumsum(hits, axis=0) - hits
    slot = jnp.sum(earlier * hits, axis=1)
    slots = (slot[:, None] == jnp.arange(capacity, dtype=jnp.int32)[None, :]).astype(jnp.int32)
    requests = jnp.sum((hits * row_steps[:, None])[:, :, None] * slots[:, None, :], axis=0)
    wanted = lax.all_to_all(requests, "agent", split_axis=0, concat_axis=0, tiled=True)
    outgoing = embedded[wanted.reshape(-1)].reshape(blocks, capacity, agents, width)
    arrived = lax.all_to_all(outgoing, "agent", split_axis=0, concat_axis=0, tiled=True)
    return arrived.reshape(blocks * capacity, agents, width), peers * capacity + slot


LEAD = 4
QUERY_STEPS = 4


def row_gather_kernel(
    head, x_ref, mine_ref, theirs_ref, proj, merge, tproj, tmerge, weight_ref,
    done_ref, reward_ref, boot_ref, values_ref, adv_ref,
    row, yout, yin, res_ref, q_ref, kv_ref, mix_ref, edge_out, edge_in,
    send_sem, recv_sem, ysend, yrecv, kvsend, kvrecv, edge_sem, go_sem,
):
    agents, width = x_ref.shape[1:]
    tm = lax.axis_index("tm")
    earlier, later = tm > 0, tm < lax.axis_size("tm") - 1
    steps = x_ref.shape[0]
    listing = mine_ref.shape[1]
    lines = row.shape[0]
    me = lax.axis_index("agent")
    y = lax.rem(me, 2)
    z = lax.div(me, 2)
    across = me + 1 - 2 * y
    has_up, has_down = z < lines - 1, z > 0
    up, down = {"agent": me + 2}, {"agent": me - 2}

    barrier = pltpu.get_barrier_semaphore()
    pl.semaphore_signal(barrier, inc=1, device_id={"agent": across}, device_id_type=MESH)

    @pl.when(has_up)
    def _():
        pl.semaphore_signal(barrier, inc=1, device_id=up, device_id_type=MESH)

    @pl.when(has_down)
    def _():
        pl.semaphore_signal(barrier, inc=1, device_id=down, device_id_type=MESH)

    @pl.when(earlier)
    def _():
        pl.semaphore_signal(barrier, inc=1, device_id={"tm": tm - 1}, device_id_type=MESH)

    @pl.when(later)
    def _():
        pl.semaphore_signal(barrier, inc=1, device_id={"tm": tm + 1}, device_id_type=MESH)

    friends = [has_up, has_down, earlier, later]
    pl.semaphore_wait(barrier, 1 + sum(friend.astype(jnp.int32) for friend in friends))

    def hop(way, h, c, own=False):
        origin = z - h if way == 0 else z + h
        return pltpu.make_async_remote_copy(
            src_ref=x_ref.at[c] if own else row.at[origin, c],
            dst_ref=row.at[origin, c],
            send_sem=send_sem.at[way, h, c],
            recv_sem=recv_sem.at[way, h, c],
            device_id=up if way == 0 else down,
            device_id_type=MESH,
        )

    def arrival(way, h, c):
        origin = z - h if way == 0 else z + h
        return pltpu.make_async_remote_copy(
            src_ref=row.at[origin, c],
            dst_ref=row.at[origin, c],
            send_sem=send_sem.at[way, h - 1, c],
            recv_sem=recv_sem.at[way, h - 1, c],
            device_id={"agent": across},
            device_id_type=MESH,
        )

    def crossing(c):
        return pltpu.make_async_remote_copy(
            src_ref=yout.at[c],
            dst_ref=yin.at[c],
            send_sem=ysend.at[c],
            recv_sem=yrecv.at[c],
            device_id={"agent": across},
            device_id_type=MESH,
        )

    def held(way, h):
        return z >= h if way == 0 else z + h < lines

    def sends(way, h):
        return held(way, h) & (has_up if way == 0 else has_down)

    def start_own(c):
        for way in range(2):
            @pl.when(sends(way, 0) & (c < steps))
            def _(way=way):
                hop(way, 0, c, own=True).start()

    def kv_copy(t):
        return pltpu.make_async_remote_copy(
            src_ref=kv_ref.at[steps + t],
            dst_ref=kv_ref.at[t],
            send_sem=kvsend.at[t],
            recv_sem=kvrecv.at[t],
            device_id={"tm": lax.rem(tm + 1, lax.axis_size("tm"))},
            device_id_type=MESH,
        )

    def edge_copy():
        count = lax.axis_size("tm")
        return pltpu.make_async_remote_copy(
            src_ref=edge_out,
            dst_ref=edge_in,
            send_sem=edge_sem.at[0],
            recv_sem=edge_sem.at[1],
            device_id={"tm": lax.rem(tm + count - 1, count)},
            device_id_type=MESH,
        )

    def fill(t, _):
        row[z, t] = x_ref[t]

        @pl.when(jnp.logical_not(earlier))
        def _():
            kv_ref[t] = jnp.zeros(kv_ref.shape[1:], kv_ref.dtype)

        return 0

    lax.fori_loop(0, steps, fill, 0)

    @pl.when(earlier)
    def _():
        pl.semaphore_wait(go_sem, 1)

    for c in range(LEAD):
        start_own(c)

    oct_, qs = 8, QUERY_STEPS
    ks = qs + steps
    coef = head**-0.5 * math.log2(math.e)

    def halves(block):
        block = block.astype(jnp.float32)
        return [
            block[:, h : h + oct_].reshape(-1, block.shape[-1]).astype(jnp.bfloat16)
            for h in (0, oct_)
        ]

    def time_chunk(q0):
        r = lax.broadcasted_iota(jnp.int32, (qs * oct_, ks * oct_), 0)
        c = lax.broadcasted_iota(jnp.int32, (qs * oct_, ks * oct_), 1)
        ahead = c // oct_ - r // oct_
        seen = (ahead > 0) & (ahead <= WINDOW) & ((q0 + c // oct_ >= steps) | earlier)
        bias = jnp.where(seen & (r % oct_ == c % oct_), 0.0, NEG).astype(jnp.float32)
        bias = jnp.concatenate([bias, bias], axis=0)

        def group(i, _):
            at = pl.ds(pl.multiple_of(i * 2 * oct_, 2 * oct_), 2 * oct_)
            for lo in range(0, width, 2 * head):
                hi = lo + 2 * head
                q = halves(q_ref[pl.ds(q0, qs), at, lo:hi])
                k = halves(kv_ref[pl.ds(q0, ks), at, lo:hi])
                v = halves(kv_ref[pl.ds(q0, ks), at, width + lo : width + hi])
                outs = [
                    pair_attention(q[h], k[h], v[h], head, coef, bias).reshape(qs, oct_, hi - lo)
                    for h in range(2)
                ]
                mix_ref[:, at, lo:hi] = jnp.concatenate(outs, axis=1).astype(jnp.bfloat16)
            return 0

        lax.fori_loop(0, agents // (2 * oct_), group, 0)
        mixed = dot(mix_ref[...].reshape(qs * agents, width), tmerge[...])
        lanes = 128
        for j in range(qs):
            res = res_ref[q0 + j] + mixed[j * agents : (j + 1) * agents]
            square, scaled = res * res, res * weight_ref[...]
            sq = sum(square[:, lo : lo + lanes] for lo in range(0, width, lanes))
            sc = sum(scaled[:, lo : lo + lanes] for lo in range(0, width, lanes))
            mean = jnp.sum(sq.T, axis=0, keepdims=True) / width
            value = jnp.sum(sc.T, axis=0, keepdims=True) * lax.rsqrt(mean + epsilon)
            values_ref[pl.ds(q0 + j, 1), :] = value

    def pick(idx, t, other):
        for zz in range(lines):
            other = jnp.where(idx == 2 * zz + y, row[zz, t], other)
        return other

    def iteration(i, _):
        start_own(i + LEAD)
        for h in range(1, lines):
            c = i - h
            for way in range(2):
                @pl.when((c >= 0) & (c < steps) & held(way, h))
                def _(way=way, h=h, c=c):
                    arrival(way, h, c).wait_recv()

                if h < lines - 1:
                    @pl.when((c >= 0) & (c < steps) & sends(way, h))
                    def _(way=way, h=h, c=c):
                        hop(way, h, c).start()
        c = i - (lines - 1)

        @pl.when((c >= 0) & (c < steps))
        def _():
            for j in range(listing):
                yout[c, j] = pick(theirs_ref[c, j], c, row[0, c])
            crossing(c).start()

        t = i - lines

        @pl.when((t >= 0) & (t < steps))
        def _():
            @pl.when(later & (t > 0))
            def _():
                kv_copy(t - 1).start()

            crossing(t).wait_recv()
            listed = [pick(mine_ref[t, j], t, yin[t, j]) for j in range(listing)]
            res, qkv = agent_step(x_ref[t], jnp.concatenate(listed, axis=0), proj, merge, tproj, head)
            res_ref[t] = res
            q_ref[t] = qkv[:, :width]
            kv_ref[steps + t] = qkv[:, width:]

            @pl.when(earlier & (t == 0))
            def _():
                def ready(s, _):
                    kv_copy(s).wait_recv()
                    return 0

                lax.fori_loop(0, steps, ready, 0)

            @pl.when(lax.rem(t, qs) == qs - 1)
            def _():
                time_chunk(t - (qs - 1))

        @pl.when(later & (i == steps - LEAD))
        def _():
            pl.semaphore_signal(go_sem, inc=1, device_id={"tm": tm + 1}, device_id_type=MESH)

        return 0

    lax.fori_loop(0, steps + lines, iteration, 0)

    @pl.when(later)
    def _():
        kv_copy(steps - 1).start()
        edge_copy().wait_recv()
        edge_out[...] = edge_in[...]

    @pl.when(jnp.logical_not(later))
    def _():
        edge_out[0:1, :] = boot_ref[...]
        edge_out[1:2, :] = jnp.zeros_like(boot_ref)

    value, running = edge_out[0:1, :], edge_out[1:2, :]
    rows = []
    for t in reversed(range(steps)):
        living = 1.0 - done_ref[t : t + 1, :].astype(jnp.float32)
        following, value = value, values_ref[t : t + 1, :]
        change = reward_ref[t : t + 1, :] + discount * living * following - value
        running = change + discount * trace_decay * living * running
        rows.append(running)
    edge_out[0:1, :] = value
    edge_out[1:2, :] = running
    for t in range(steps):
        adv_ref[t : t + 1, :] = rows[steps - 1 - t]

    @pl.when(earlier)
    def _():
        edge_copy().start()

    def drain(c, _):
        crossing(c).wait_send()

        @pl.when(later)
        def _():
            kv_copy(c).wait_send()

        for way in range(2):
            for h in range(lines - 1):
                @pl.when(sends(way, h))
                def _(way=way, h=h):
                    hop(way, h, c, own=h == 0).wait_send()
        return 0

    lax.fori_loop(0, steps, drain, 0)

    @pl.when(earlier)
    def _():
        edge_copy().wait_send()


def row_gather_call(
    embedded, mine, theirs, proj, merge, tproj, tmerge, weight, done, rewards, bootstrap, head
):
    steps, agents, width = embedded.shape
    lines = lax.axis_size("agent") // 2
    listing = mine.shape[1]
    vmem, smem = pl.BlockSpec(memory_space=pltpu.VMEM), pl.BlockSpec(memory_space=pltpu.SMEM)
    dma = pltpu.SemaphoreType.DMA
    out = jax.ShapeDtypeStruct((steps, agents), jnp.float32)
    return pl.pallas_call(
        functools.partial(row_gather_kernel, head),
        in_specs=[vmem, smem, smem] + [vmem] * 8,
        out_specs=[vmem, vmem],
        out_shape=[out, out],
        scratch_shapes=[
            pltpu.VMEM((lines, steps, agents, width), jnp.bfloat16),
            pltpu.VMEM((steps, listing, agents, width), jnp.bfloat16),
            pltpu.VMEM((steps, listing, agents, width), jnp.bfloat16),
            pltpu.VMEM((steps, agents, width), jnp.float32),
            pltpu.VMEM((steps, agents, width), jnp.bfloat16),
            pltpu.VMEM((2 * steps, agents, 2 * width), jnp.bfloat16),
            pltpu.VMEM((QUERY_STEPS, agents, width), jnp.bfloat16),
            pltpu.VMEM((2, agents), jnp.float32),
            pltpu.VMEM((2, agents), jnp.float32),
            dma((2, lines - 1, steps)),
            dma((2, lines - 1, steps)),
            dma((steps,)),
            dma((steps,)),
            dma((steps,)),
            dma((steps,)),
            dma((2,)),
            pltpu.SemaphoreType.REGULAR,
        ],
        compiler_params=pltpu.CompilerParams(
            collective_id=0, has_side_effects=True, vmem_limit_bytes=58 * 2**20
        ),
        name="critic_layer",
    )(
        embedded, mine, theirs, proj, merge, tproj, tmerge, weight.reshape(1, width),
        done, rewards, bootstrap.reshape(1, agents),
    )


def body(
    embedded,
    block_lists,
    done_flags,
    rewards,
    bootstrap,
    agent_proj,
    agent_merge,
    time_proj,
    time_merge,
    value_weight,
):
    steps, agents, width = embedded.shape
    head = width // HEADS
    assert steps == WINDOW
    blocks = lax.axis_size("agent")
    gathered = (blocks // 2) * steps * agents * width * 2
    if blocks % 2 == 0 and blocks > 2 and gathered <= 12 * 2**20:
        theirs = lax.ppermute(block_lists[0], "agent", [(i, i ^ 1) for i in range(blocks)])
        values, advantages = row_gather_call(
            embedded, block_lists[0], theirs, agent_proj, agent_merge, time_proj, time_merge,
            value_weight, done_flags, rewards, bootstrap, head,
        )
        return (values, advantages)
    arrived, positions = exchange(embedded, block_lists)
    res, qkv = agent_call(embedded, arrived, positions, agent_proj, agent_merge, time_proj, head)
    prev = from_behind(qkv[:, :, width:], "tm", 1)
    values = time_call(res, qkv, prev, time_merge, value_weight, head)
    return (values, advantage_pass(values, done_flags, rewards, bootstrap))


def solution(mesh):
    placed = (
        P(("groups", "tm"), "agent", None),
        P(("groups", "agent"), "tm", None),
        P(("groups", "tm"), "agent"),
        P(("groups", "tm"), "agent"),
        P(("groups", "agent")),
        P(),
        P(),
        P(),
        P(),
        P(),
    )
    return jax.shard_map(
        body,
        mesh=mesh,
        in_specs=placed,
        out_specs=(P(("groups", "tm"), "agent"), P(("groups", "tm"), "agent")),
        check_vma=False,
    )
```

```python
import functools
import math

import jax
import jax.numpy as jnp
from jax import lax
from jax.experimental import pallas as pl
from jax.experimental.pallas import tpu as pltpu
from jax.sharding import PartitionSpec as P

HEADS = 8
WINDOW = 16

discount = 0.9997
trace_decay = 0.995
epsilon = 1e-06
NEG = -1e30
MESH = pl.DeviceIdType.MESH


def normed_bf16(x):
    return (x * lax.rsqrt(jnp.mean(x * x, axis=-1, keepdims=True) + epsilon)).astype(jnp.bfloat16)


def dot(a, b):
    return jnp.dot(a, b, preferred_element_type=jnp.float32)


def pair_attention(q, k, v, head, coef, bias=None):
    rows = q.shape[0]
    first = lax.broadcasted_iota(jnp.int32, q.shape, 1) < head
    zero = jnp.zeros_like(q)
    both = jnp.concatenate([jnp.where(first, q, zero), jnp.where(first, zero, q)], axis=0)
    s = lax.dot_general(both, k, (((1,), (1,)), ((), ())), preferred_element_type=jnp.float32)
    s = s * coef
    if bias is not None:
        s = s + bias
    e = jnp.exp2(s - jnp.max(s, axis=-1, keepdims=True))
    o = dot(e.astype(jnp.bfloat16), v) / jnp.sum(e, axis=-1, keepdims=True)
    return jnp.where(first, o[:rows], o[rows:])


def agent_step(x, listed, proj_ref, merge_ref, tproj_ref, head):
    width = x.shape[-1]
    coef = head**-0.5 * math.log2(math.e)
    x = x.astype(jnp.float32)
    own = dot(normed_bf16(x), proj_ref[...]).astype(jnp.bfloat16)
    other = dot(normed_bf16(listed.astype(jnp.float32)), proj_ref[:, width:]).astype(jnp.bfloat16)
    outs = []
    for lo in range(0, width, 2 * head):
        hi = lo + 2 * head
        k = jnp.concatenate([own[:, width + lo : width + hi], other[:, lo:hi]], axis=0)
        v = jnp.concatenate(
            [own[:, 2 * width + lo : 2 * width + hi], other[:, width + lo : width + hi]], axis=0
        )
        outs.append(pair_attention(own[:, lo:hi], k, v, head, coef))
    mix = jnp.concatenate(outs, axis=1).astype(jnp.bfloat16)
    res = x + dot(mix, merge_ref[...])
    return res, dot(normed_bf16(res), tproj_ref[...]).astype(jnp.bfloat16)


def agent_kernel(head, listing, pos, x_ref, *refs):
    listed = [r[0] for r in refs[:listing]]
    proj, merge, tproj, res_ref, qkv_ref = refs[listing:]
    res, qkv = agent_step(x_ref[0], jnp.concatenate(listed, axis=0), proj, merge, tproj, head)
    res_ref[0] = res
    qkv_ref[0] = qkv


def agent_call(embedded, arrived, positions, proj, merge, tproj, head):
    steps, agents, width = embedded.shape
    listing = positions.shape[0] // steps
    block = (1, agents, width)
    whole = lambda a: pl.BlockSpec(a.shape, lambda t, p: (0, 0))
    pick = lambda j: pl.BlockSpec(block, lambda t, p: (p[t * listing + j], 0, 0))
    return pl.pallas_call(
        functools.partial(agent_kernel, head, listing),
        grid_spec=pltpu.PrefetchScalarGridSpec(
            num_scalar_prefetch=1,
            grid=(steps,),
            in_specs=[pl.BlockSpec(block, lambda t, p: (t, 0, 0))]
            + [pick(j) for j in range(listing)]
            + [whole(proj), whole(merge), whole(tproj)],
            out_specs=[
                pl.BlockSpec(block, lambda t, p: (t, 0, 0)),
                pl.BlockSpec((1, agents, 3 * width), lambda t, p: (t, 0, 0)),
            ],
        ),
        out_shape=[
            jax.ShapeDtypeStruct((steps, agents, width), jnp.float32),
            jax.ShapeDtypeStruct((steps, agents, 3 * width), jnp.bfloat16),
        ],
        compiler_params=pltpu.CompilerParams(vmem_limit_bytes=40 * 2**20),
        name="agent_attention",
    )(positions, embedded, *([arrived] * listing), proj, merge, tproj)


def time_kernel(head, res_ref, qkv_ref, prev_ref, merge_ref, weight_ref, out_ref, mix_ref):
    steps, agents, width = res_ref.shape
    coef = head**-0.5 * math.log2(math.e)
    oct_ = 8
    rows, cols = steps * oct_, 2 * steps * oct_
    r = lax.broadcasted_iota(jnp.int32, (rows, cols), 0)
    c = lax.broadcasted_iota(jnp.int32, (rows, cols), 1)
    qt, ks = r // oct_, c // oct_ - steps
    seen = (ks <= qt) & (ks > qt - WINDOW) & ((ks >= 0) | (lax.axis_index("tm") > 0))
    bias = jnp.where(seen & (r % oct_ == c % oct_), 0.0, NEG).astype(jnp.float32)
    bias = jnp.concatenate([bias, bias], axis=0)

    def halves(block):
        block = block.astype(jnp.float32)
        return [
            block[:, h : h + oct_].reshape(steps * oct_, block.shape[-1]).astype(jnp.bfloat16)
            for h in (0, oct_)
        ]

    def group(i, _):
        at = pl.ds(pl.multiple_of(i * 2 * oct_, 2 * oct_), 2 * oct_)
        for lo in range(0, width, 2 * head):
            hi = lo + 2 * head
            q = halves(qkv_ref[:, at, lo:hi])
            k0 = halves(prev_ref[:, at, lo:hi])
            k1 = halves(qkv_ref[:, at, width + lo : width + hi])
            v0 = halves(prev_ref[:, at, width + lo : width + hi])
            v1 = halves(qkv_ref[:, at, 2 * width + lo : 2 * width + hi])
            outs = []
            for h in range(2):
                k = jnp.concatenate([k0[h], k1[h]], axis=0)
                v = jnp.concatenate([v0[h], v1[h]], axis=0)
                o = pair_attention(q[h], k, v, head, coef, bias)
                outs.append(o.reshape(steps, oct_, hi - lo))
            mix_ref[:, at, lo:hi] = jnp.concatenate(outs, axis=1).astype(jnp.bfloat16)
        return 0

    lax.fori_loop(0, agents // (2 * oct_), group, 0)

    def finish(t, _):
        res = res_ref[t] + dot(mix_ref[t], merge_ref[...])
        square = res * res
        scaled = res * weight_ref[...]
        lanes = 128
        sq = sum(square[:, j : j + lanes] for j in range(0, width, lanes))
        sc = sum(scaled[:, j : j + lanes] for j in range(0, width, lanes))
        mean = jnp.sum(sq.T, axis=0, keepdims=True) / width
        out_ref[pl.ds(t, 1), :] = jnp.sum(sc.T, axis=0, keepdims=True) * lax.rsqrt(mean + epsilon)
        return 0

    lax.fori_loop(0, steps, finish, 0)


def time_call(res, qkv, prev, merge, weight, head):
    steps, agents, width = res.shape
    return pl.pallas_call(
        functools.partial(time_kernel, head),
        out_shape=jax.ShapeDtypeStruct((steps, agents), jnp.float32),
        in_specs=[pl.BlockSpec(memory_space=pltpu.VMEM)] * 5,
        out_specs=pl.BlockSpec(memory_space=pltpu.VMEM),
        scratch_shapes=[pltpu.VMEM((steps, agents, width), jnp.bfloat16)],
        compiler_params=pltpu.CompilerParams(vmem_limit_bytes=56 * 2**20),
        name="time_attention",
    )(res, qkv, prev, merge, weight.reshape(1, width))


def from_behind(value, axis, by):
    devices = lax.axis_size(axis)
    pairs = [(i, i + by) for i in range(devices) if 0 <= i + by < devices]
    return lax.ppermute(value, axis, pairs)


def advantage_pass(values, done_flags, rewards, bootstrap):
    steps = values.shape[0]
    parts = lax.axis_size("tm")
    last = lax.axis_index("tm") == parts - 1
    living = 1.0 - done_flags.astype(jnp.float32)
    factors = discount * trace_decay * living

    def run(following_last, running):
        following = jnp.concatenate([values[1:], following_last[None]], axis=0)
        changes = rewards + discount * living * following - values
        rows = [None] * steps
        for t in reversed(range(steps)):
            running = changes[t] + factors[t] * running
            rows[t] = running
        return jnp.stack(rows)

    zero = jnp.zeros_like(bootstrap)
    advantages = run(bootstrap, zero)
    for _ in range(parts - 1):
        sent = jnp.stack([values[0], advantages[0]])
        got = from_behind(sent, "tm", -1)
        advantages = run(jnp.where(last, bootstrap, got[0]), jnp.where(last, zero, got[1]))
    return advantages


def exchange(embedded, block_lists):
    steps, agents, width = embedded.shape
    listing = block_lists.shape[2]
    blocks = lax.axis_size("agent")
    capacity = max(2, (2 * steps * listing + blocks - 1) // blocks)
    peers = block_lists[0].reshape(-1)
    count = peers.shape[0]
    row_steps = jnp.arange(count, dtype=jnp.int32) // listing
    hits = (peers[:, None] == jnp.arange(blocks, dtype=jnp.int32)[None, :]).astype(jnp.int32)
    earlier = jnp.cumsum(hits, axis=0) - hits
    slot = jnp.sum(earlier * hits, axis=1)
    slots = (slot[:, None] == jnp.arange(capacity, dtype=jnp.int32)[None, :]).astype(jnp.int32)
    requests = jnp.sum((hits * row_steps[:, None])[:, :, None] * slots[:, None, :], axis=0)
    wanted = lax.all_to_all(requests, "agent", split_axis=0, concat_axis=0, tiled=True)
    outgoing = embedded[wanted.reshape(-1)].reshape(blocks, capacity, agents, width)
    arrived = lax.all_to_all(outgoing, "agent", split_axis=0, concat_axis=0, tiled=True)
    return arrived.reshape(blocks * capacity, agents, width), peers * capacity + slot


LEAD = 4
QUERY_STEPS = 16


def row_gather_kernel(
    head, x_ref, mine_ref, theirs_ref, proj, merge, tproj, tmerge, weight_ref,
    done_ref, reward_ref, boot_ref, values_ref, adv_ref,
    row, yout, yin, res_ref, q_ref, kv_ref, mix_ref, edge_out, edge_in,
    send_sem, recv_sem, ysend, yrecv, kvsend, kvrecv, edge_sem,
):
    agents, width = x_ref.shape[1:]
    tm = lax.axis_index("tm")
    earlier, later = tm > 0, tm < lax.axis_size("tm") - 1
    steps = x_ref.shape[0]
    listing = mine_ref.shape[1]
    lines = row.shape[0]
    me = lax.axis_index("agent")
    y = lax.rem(me, 2)
    z = lax.div(me, 2)
    across = me + 1 - 2 * y
    has_up, has_down = z < lines - 1, z > 0
    up, down = {"agent": me + 2}, {"agent": me - 2}

    barrier = pltpu.get_barrier_semaphore()
    pl.semaphore_signal(barrier, inc=1, device_id={"agent": across}, device_id_type=MESH)

    @pl.when(has_up)
    def _():
        pl.semaphore_signal(barrier, inc=1, device_id=up, device_id_type=MESH)

    @pl.when(has_down)
    def _():
        pl.semaphore_signal(barrier, inc=1, device_id=down, device_id_type=MESH)

    @pl.when(earlier)
    def _():
        pl.semaphore_signal(barrier, inc=1, device_id={"tm": tm - 1}, device_id_type=MESH)

    @pl.when(later)
    def _():
        pl.semaphore_signal(barrier, inc=1, device_id={"tm": tm + 1}, device_id_type=MESH)

    friends = [has_up, has_down, earlier, later]
    pl.semaphore_wait(barrier, 1 + sum(friend.astype(jnp.int32) for friend in friends))

    def hop(way, h, c, own=False):
        origin = z - h if way == 0 else z + h
        return pltpu.make_async_remote_copy(
            src_ref=x_ref.at[c] if own else row.at[origin, c],
            dst_ref=row.at[origin, c],
            send_sem=send_sem.at[way, h, c],
            recv_sem=recv_sem.at[way, h, c],
            device_id=up if way == 0 else down,
            device_id_type=MESH,
        )

    def arrival(way, h, c):
        origin = z - h if way == 0 else z + h
        return pltpu.make_async_remote_copy(
            src_ref=row.at[origin, c],
            dst_ref=row.at[origin, c],
            send_sem=send_sem.at[way, h - 1, c],
            recv_sem=recv_sem.at[way, h - 1, c],
            device_id={"agent": across},
            device_id_type=MESH,
        )

    def crossing(c):
        return pltpu.make_async_remote_copy(
            src_ref=yout.at[c],
            dst_ref=yin.at[c],
            send_sem=ysend.at[c],
            recv_sem=yrecv.at[c],
            device_id={"agent": across},
            device_id_type=MESH,
        )

    def held(way, h):
        return z >= h if way == 0 else z + h < lines

    def sends(way, h):
        return held(way, h) & (has_up if way == 0 else has_down)

    def start_own(c):
        for way in range(2):
            @pl.when(sends(way, 0) & (c < steps))
            def _(way=way):
                hop(way, 0, c, own=True).start()

    def kv_copy(t):
        return pltpu.make_async_remote_copy(
            src_ref=kv_ref.at[steps + t],
            dst_ref=kv_ref.at[t],
            send_sem=kvsend.at[t],
            recv_sem=kvrecv.at[t],
            device_id={"tm": lax.rem(tm + 1, lax.axis_size("tm"))},
            device_id_type=MESH,
        )

    def edge_copy():
        count = lax.axis_size("tm")
        return pltpu.make_async_remote_copy(
            src_ref=edge_out,
            dst_ref=edge_in,
            send_sem=edge_sem.at[0],
            recv_sem=edge_sem.at[1],
            device_id={"tm": lax.rem(tm + count - 1, count)},
            device_id_type=MESH,
        )

    def fill(t, _):
        row[z, t] = x_ref[t]

        @pl.when(jnp.logical_not(earlier))
        def _():
            kv_ref[t] = jnp.zeros(kv_ref.shape[1:], kv_ref.dtype)

        return 0

    lax.fori_loop(0, steps, fill, 0)

    for c in range(LEAD):
        start_own(c)

    oct_, qs = 8, QUERY_STEPS
    ks = qs + steps
    coef = head**-0.5 * math.log2(math.e)

    def halves(block):
        block = block.astype(jnp.float32)
        return [
            block[:, h : h + oct_].reshape(-1, block.shape[-1]).astype(jnp.bfloat16)
            for h in (0, oct_)
        ]

    def time_chunk(q0):
        r = lax.broadcasted_iota(jnp.int32, (qs * oct_, ks * oct_), 0)
        c = lax.broadcasted_iota(jnp.int32, (qs * oct_, ks * oct_), 1)
        ahead = c // oct_ - r // oct_
        seen = (ahead > 0) & (ahead <= WINDOW) & ((q0 + c // oct_ >= steps) | earlier)
        bias = jnp.where(seen & (r % oct_ == c % oct_), 0.0, NEG).astype(jnp.float32)
        bias = jnp.concatenate([bias, bias], axis=0)

        def group(i, _):
            at = pl.ds(pl.multiple_of(i * 2 * oct_, 2 * oct_), 2 * oct_)
            for lo in range(0, width, 2 * head):
                hi = lo + 2 * head
                q = halves(q_ref[pl.ds(q0, qs), at, lo:hi])
                k = halves(kv_ref[pl.ds(q0, ks), at, lo:hi])
                v = halves(kv_ref[pl.ds(q0, ks), at, width + lo : width + hi])
                outs = [
                    pair_attention(q[h], k[h], v[h], head, coef, bias).reshape(qs, oct_, hi - lo)
                    for h in range(2)
                ]
                mix_ref[:, at, lo:hi] = jnp.concatenate(outs, axis=1).astype(jnp.bfloat16)
            return 0

        lax.fori_loop(0, agents // (2 * oct_), group, 0)
        mixed = dot(mix_ref[...].reshape(qs * agents, width), tmerge[...])
        lanes = 128
        for j in range(qs):
            res = res_ref[q0 + j] + mixed[j * agents : (j + 1) * agents]
            square, scaled = res * res, res * weight_ref[...]
            sq = sum(square[:, lo : lo + lanes] for lo in range(0, width, lanes))
            sc = sum(scaled[:, lo : lo + lanes] for lo in range(0, width, lanes))
            mean = jnp.sum(sq.T, axis=0, keepdims=True) / width
            value = jnp.sum(sc.T, axis=0, keepdims=True) * lax.rsqrt(mean + epsilon)
            values_ref[pl.ds(q0 + j, 1), :] = value

    def pick(idx, t, other):
        for zz in range(lines):
            other = jnp.where(idx == 2 * zz + y, row[zz, t], other)
        return other

    def iteration(i, _):
        start_own(i + LEAD)
        for h in range(1, lines):
            c = i - h
            for way in range(2):
                @pl.when((c >= 0) & (c < steps) & held(way, h))
                def _(way=way, h=h, c=c):
                    arrival(way, h, c).wait_recv()

                if h < lines - 1:
                    @pl.when((c >= 0) & (c < steps) & sends(way, h))
                    def _(way=way, h=h, c=c):
                        hop(way, h, c).start()
        c = i - (lines - 1)

        @pl.when((c >= 0) & (c < steps))
        def _():
            for j in range(listing):
                yout[c, j] = pick(theirs_ref[c, j], c, row[0, c])
            crossing(c).start()

        t = i - lines

        @pl.when((t >= 0) & (t < steps))
        def _():
            @pl.when(later & (t > 0))
            def _():
                kv_copy(t - 1).start()

            crossing(t).wait_recv()
            listed = [pick(mine_ref[t, j], t, yin[t, j]) for j in range(listing)]
            res, qkv = agent_step(x_ref[t], jnp.concatenate(listed, axis=0), proj, merge, tproj, head)
            res_ref[t] = res
            q_ref[t] = qkv[:, :width]
            kv_ref[steps + t] = qkv[:, width:]

            @pl.when(jnp.logical_not(earlier) & (lax.rem(t, qs) == qs - 1))
            def _():
                time_chunk(t - (qs - 1))

        return 0

    lax.fori_loop(0, steps + lines, iteration, 0)

    @pl.when(later)
    def _():
        kv_copy(steps - 1).start()

    @pl.when(earlier)
    def _():
        def ready(s, _):
            kv_copy(s).wait_recv()
            return 0

        lax.fori_loop(0, steps, ready, 0)

        def chunk(n, _):
            time_chunk(n * qs)
            return 0

        lax.fori_loop(0, steps // qs, chunk, 0)

    @pl.when(later)
    def _():
        edge_copy().wait_recv()
        edge_out[...] = edge_in[...]

    @pl.when(jnp.logical_not(later))
    def _():
        edge_out[0:1, :] = boot_ref[...]
        edge_out[1:2, :] = jnp.zeros_like(boot_ref)

    value, running = edge_out[0:1, :], edge_out[1:2, :]
    rows = []
    for t in reversed(range(steps)):
        living = 1.0 - done_ref[t : t + 1, :].astype(jnp.float32)
        following, value = value, values_ref[t : t + 1, :]
        change = reward_ref[t : t + 1, :] + discount * living * following - value
        running = change + discount * trace_decay * living * running
        rows.append(running)
    edge_out[0:1, :] = value
    edge_out[1:2, :] = running
    for t in range(steps):
        adv_ref[t : t + 1, :] = rows[steps - 1 - t]

    @pl.when(earlier)
    def _():
        edge_copy().start()

    def drain(c, _):
        crossing(c).wait_send()

        @pl.when(later)
        def _():
            kv_copy(c).wait_send()

        for way in range(2):
            for h in range(lines - 1):
                @pl.when(sends(way, h))
                def _(way=way, h=h):
                    hop(way, h, c, own=h == 0).wait_send()
        return 0

    lax.fori_loop(0, steps, drain, 0)

    @pl.when(earlier)
    def _():
        edge_copy().wait_send()


def row_gather_call(
    embedded, mine, theirs, proj, merge, tproj, tmerge, weight, done, rewards, bootstrap, head
):
    steps, agents, width = embedded.shape
    lines = lax.axis_size("agent") // 2
    listing = mine.shape[1]
    vmem, smem = pl.BlockSpec(memory_space=pltpu.VMEM), pl.BlockSpec(memory_space=pltpu.SMEM)
    dma = pltpu.SemaphoreType.DMA
    out = jax.ShapeDtypeStruct((steps, agents), jnp.float32)
    return pl.pallas_call(
        functools.partial(row_gather_kernel, head),
        in_specs=[vmem, smem, smem] + [vmem] * 8,
        out_specs=[vmem, vmem],
        out_shape=[out, out],
        scratch_shapes=[
            pltpu.VMEM((lines, steps, agents, width), jnp.bfloat16),
            pltpu.VMEM((steps, listing, agents, width), jnp.bfloat16),
            pltpu.VMEM((steps, listing, agents, width), jnp.bfloat16),
            pltpu.VMEM((steps, agents, width), jnp.float32),
            pltpu.VMEM((steps, agents, width), jnp.bfloat16),
            pltpu.VMEM((2 * steps, agents, 2 * width), jnp.bfloat16),
            pltpu.VMEM((QUERY_STEPS, agents, width), jnp.bfloat16),
            pltpu.VMEM((2, agents), jnp.float32),
            pltpu.VMEM((2, agents), jnp.float32),
            dma((2, lines - 1, steps)),
            dma((2, lines - 1, steps)),
            dma((steps,)),
            dma((steps,)),
            dma((steps,)),
            dma((steps,)),
            dma((2,)),
        ],
        compiler_params=pltpu.CompilerParams(
            collective_id=0, has_side_effects=True, vmem_limit_bytes=58 * 2**20
        ),
        name="critic_layer",
    )(
        embedded, mine, theirs, proj, merge, tproj, tmerge, weight.reshape(1, width),
        done, rewards, bootstrap.reshape(1, agents),
    )


def body(
    embedded,
    block_lists,
    done_flags,
    rewards,
    bootstrap,
    agent_proj,
    agent_merge,
    time_proj,
    time_merge,
    value_weight,
):
    steps, agents, width = embedded.shape
    head = width // HEADS
    assert steps == WINDOW
    blocks = lax.axis_size("agent")
    gathered = (blocks // 2) * steps * agents * width * 2
    if blocks % 2 == 0 and blocks > 2 and gathered <= 12 * 2**20:
        theirs = lax.ppermute(block_lists[0], "agent", [(i, i ^ 1) for i in range(blocks)])
        values, advantages = row_gather_call(
            embedded, block_lists[0], theirs, agent_proj, agent_merge, time_proj, time_merge,
            value_weight, done_flags, rewards, bootstrap, head,
        )
        return (values, advantages)
    arrived, positions = exchange(embedded, block_lists)
    res, qkv = agent_call(embedded, arrived, positions, agent_proj, agent_merge, time_proj, head)
    prev = from_behind(qkv[:, :, width:], "tm", 1)
    values = time_call(res, qkv, prev, time_merge, value_weight, head)
    return (values, advantage_pass(values, done_flags, rewards, bootstrap))


def solution(mesh):
    placed = (
        P(("groups", "tm"), "agent", None),
        P(("groups", "agent"), "tm", None),
        P(("groups", "tm"), "agent"),
        P(("groups", "tm"), "agent"),
        P(("groups", "agent")),
        P(),
        P(),
        P(),
        P(),
        P(),
    )
    return jax.shard_map(
        body,
        mesh=mesh,
        in_specs=placed,
        out_specs=(P(("groups", "tm"), "agent"), P(("groups", "tm"), "agent")),
        check_vma=False,
    )
```
